128 devices in a mesh: stn: 64 (over z, y, x_hi, core), tm: 2 (over x_lo).
Axes of the slice: x: 4 (x_hi: 2, x_lo: 2; x = x_hi * 2 + x_lo), y: 4, z: 4, core: 2. Of those that a mesh axis runs over, the one named last changes fastest.
Arguments:
- voltages: bfloat16 [2, 1024, 131072], P(None, 'stn', 'tm'), may hold values from -6 to 6
- filter_taps: float32 [16, 4096], replicated, may hold values from -1.5 to 1.5
- membership: int32 [128, 512], P('stn'), may hold values from 0 to 3
- block_active: int32 [128, 10], P('stn'), may hold values 0 or 1
Outputs:
- visibilities: float32 [128, 10, 2, 256, 256], P('stn', None, None, 'tm')
The draws below stay inside these ranges and needn't reach their ends.
All inputs are finite; a program needn't handle non-finite values. No bound on the sum of `block_active` on one device may be relied on, other than what follows from the above.
Results may differ from the reference program's by a relative error of at most 0.006.
Values may be sent and summed in bfloat16 or wider, within the bound.
No kernel may reach another device: no remote copies, remote signals or barrier semaphores. Data moves between devices by JAX's collectives and lax.ppermute only.
A program may use at most 128 MiB of HBM per device.

```python
import math
import jax
import jax.numpy as jnp
import numpy as np
from jax import lax

STATIONS = 512
INPUTS = 1024
TAPS = 16
RADIX = 64
FFT = 4096
AVG = 16
CHANNELS = 128
FINE = 2048
F_DEV = 16
FRAMES = 32
SAMPLES = 131072
BLOCK = 256
PAIRS = 10
N_TM = 2


def place_ends(entries, own_key, low, top_value):
    longest = entries.shape.index(max(entries.shape))
    spots = []
    for shift in (0, 1):
        where = [jax.random.randint(jax.random.fold_in(own_key, axis), (), 0, length) for axis, length in enumerate(entries.shape)]
        where[longest] = (where[longest] + shift) % entries.shape[longest]
        spots.append(tuple(where))
    return entries.at[spots[0]].set(low).at[spots[1]].set(top_value)


def shard_levels(rng, shape, cuts, smallest, high):
    level = 1.0
    for dim, parts in cuts:
        heights = jax.random.uniform(jax.random.fold_in(jax.random.fold_in(rng, 6), dim), (parts,), jnp.float32, smallest / len(cuts), high / len(cuts))
        level = level * jnp.repeat(jnp.exp(heights), shape[dim] // parts).reshape((-1,) + (1,) * (len(shape) - 1 - dim))
    return level


def bell_draw(own_key, shape, deviation, reach, shards=(), held_as=jnp.bfloat16):
    values = deviation * jax.random.normal(own_key, shape, jnp.float32)
    if shards:
        values = values * shard_levels(own_key, shape, shards, -0.22, 0.18)
    return jnp.clip(values, -reach, reach).astype(held_as)


def setup_inputs(seed: int = 0) -> dict:
    splits = jax.random.split(jax.random.key(seed), 5)
    voltages = bell_draw(splits[0], (2, INPUTS, SAMPLES), 1.0, 6.0, ((1, 64), (2, 2)))
    filter_taps = bell_draw(splits[1], (TAPS, FFT), TAPS ** -0.5, 1.5, (), jnp.float32)
    membership = place_ends(jax.random.randint(splits[2], (CHANNELS, STATIONS), 0, 4), jax.random.fold_in(splits[2], 1), 0, 3).astype(jnp.int32)
    block_active = place_ends((jax.random.randint(splits[3], (CHANNELS, PAIRS), 0, 2) < 1).astype(jnp.int32), jax.random.fold_in(splits[3], 1), 0, 1)
    return {"voltages": voltages, "filter_taps": filter_taps, "membership": membership, "block_active": block_active}


def pair_tables(count):
    upper_list = []
    lower_list = []
    for upper in range(count):
        for lower in range(upper + 1):
            upper_list.append(upper)
            lower_list.append(lower)
    return np.array(upper_list, dtype=np.int32), np.array(lower_list, dtype=np.int32)


def reference(voltages, filter_taps, membership, block_active):
    group_width = math.gcd(INPUTS, 32)
    group_count = INPUTS // group_width
    bins = ((np.arange(FINE) - RADIX * (FINE // (2 * RADIX))) % FFT).astype(np.int32)

    def channelize(group_index):
        group = lax.dynamic_slice_in_dim(voltages, group_index * group_width, group_width, 1)
        frames = group.astype(jnp.float32).reshape(2, group_width, FRAMES, FFT)
        padded = jnp.concatenate([jnp.zeros((2, group_width, TAPS - 1, FFT), jnp.float32), frames], axis=2)
        filtered = jnp.zeros((2, group_width, FRAMES, FFT), jnp.float32)
        for tap_index in range(TAPS):
            filtered = filtered + filter_taps[tap_index] * padded[:, :, tap_index:tap_index + FRAMES, :]
        signal = lax.complex(filtered[0], filtered[1])
        transformed = jnp.fft.fft(signal, axis=-1) / RADIX
        picked = transformed[:, :, bins]
        stacked = jnp.stack([jnp.real(picked), jnp.imag(picked)], axis=1)
        return stacked.astype(jnp.bfloat16)

    spectra = lax.map(channelize, jnp.arange(group_count, dtype=jnp.int32))
    spectra = spectra.reshape(INPUTS, 2, FRAMES, FINE)

    upper_tab, lower_tab = pair_tables(INPUTS // BLOCK)
    block_count = INPUTS // BLOCK
    scale = 1.0 / (AVG * FRAMES)

    def correlate(channel):
        piece = lax.dynamic_slice_in_dim(spectra, channel * AVG, AVG, 3)
        station_ids = lax.dynamic_index_in_dim(membership, channel, 0, keepdims=False)
        per_input = jnp.repeat(station_ids, 2)
        same = (per_input[:, None] == per_input[None, :]).astype(jnp.float32)
        active = lax.dynamic_index_in_dim(block_active, channel, 0, keepdims=False).astype(jnp.float32)
        mask = same.reshape(block_count, BLOCK, block_count, BLOCK)[upper_tab, :, lower_tab, :]
        mask = mask * active[:, None, None]
        total = jnp.zeros((PAIRS, 2, BLOCK, BLOCK), jnp.float32)
        for block_time in range(N_TM):
            part = piece[:, :, block_time * F_DEV:(block_time + 1) * F_DEV, :].astype(jnp.float32)
            real_in = part[:, 0].reshape(INPUTS, F_DEV * AVG)
            imag_in = part[:, 1].reshape(INPUTS, F_DEV * AVG)
            left = jnp.concatenate([real_in, imag_in], axis=1)
            swapped = jnp.concatenate([imag_in, -real_in], axis=1)
            real_prod = jnp.dot(left, left.T, precision=lax.Precision.HIGHEST)
            imag_prod = jnp.dot(swapped, left.T, precision=lax.Precision.HIGHEST)
            gram = jnp.stack([real_prod, imag_prod]) * scale
            picked = gram.reshape(2, block_count, BLOCK, block_count, BLOCK)[:, upper_tab, :, lower_tab, :]
            partial_value = (picked * mask[:, None]).astype(jnp.bfloat16)
            partial_value = lax.optimization_barrier(partial_value)
            total = total + partial_value.astype(jnp.float32)
        return total

    return lax.map(correlate, jnp.arange(CHANNELS, dtype=jnp.int32))
```

```python
import functools
import math

import jax
import jax.numpy as jnp
import numpy as np
from jax import lax
from jax.experimental import pallas as pl
from jax.experimental.pallas import tpu as pltpu
from jax.sharding import PartitionSpec as P

TAPS = 16
FFT = 4096
LANES = 128
ROWS = FFT // LANES
AVG = 16
F_DEV = 16
PAIRS = ((0, 0), (1, 0), (1, 1), (2, 0), (2, 1), (2, 2), (3, 0), (3, 1), (3, 2), (3, 3))
PART = 8


def tables():
    q = np.arange(ROWS)
    l = np.arange(LANES)
    angle = 2 * np.pi * np.outer(q, q) / ROWS
    one = np.block([[np.cos(angle), np.sin(angle)], [-np.sin(angle), np.cos(angle)]])
    angle = 2 * np.pi * np.outer(q, l) / FFT
    turn = np.stack([np.cos(angle), -np.sin(angle)])
    angle = 2 * np.pi * np.outer(np.arange(64) - 32, l) / LANES
    two = np.block([[np.cos(angle), np.sin(angle)], [-np.sin(angle), np.cos(angle)]]) / 64
    bf = jnp.bfloat16
    return jnp.asarray(one, bf), jnp.asarray(turn, jnp.float32), jnp.asarray(two, bf)


def spectra_kernel(tail, x_ref, taps_ref, one_ref, turn_ref, two_ref, out_ref, fir, mid, spread):
    def one_input(i, carry):
        for c in range(2):
            for q in range(0, ROWS, 8):
                x = [x_ref[c, i, m, q : q + 8, :].astype(jnp.float32) for m in range(F_DEV)]
                w = [taps_ref[t, q : q + 8, :] for t in range(TAPS)]
                for m in range(F_DEV):
                    total = None
                    for t in range(TAPS):
                        frame = m - (TAPS - 1) + t + (F_DEV if tail else 0)
                        if 0 <= frame < F_DEV:
                            term = w[t] * x[frame]
                            total = term if total is None else total + term
                    if total is None:
                        total = jnp.zeros((8, LANES), jnp.float32)
                    fir[c * ROWS + q : c * ROWS + q + 8, m * LANES : (m + 1) * LANES] = total
        for m in range(0, F_DEV, 2):
            first = jnp.dot(
                one_ref[...],
                fir[:, m * LANES : (m + 2) * LANES].astype(jnp.bfloat16),
                preferred_element_type=jnp.float32,
            )
            for k in range(2):
                re = first[:ROWS, k * LANES : (k + 1) * LANES]
                im = first[ROWS:, k * LANES : (k + 1) * LANES]
                parts = (
                    re * turn_ref[0] - im * turn_ref[1],
                    re * turn_ref[1] + im * turn_ref[0],
                )
                for c in range(2):
                    value = parts[c].astype(jnp.bfloat16)
                    for h in range(2):
                        row = h * 256 + (m + k) * AVG
                        mid[row : row + AVG, c * LANES : (c + 1) * LANES] = value[
                            h * AVG : (h + 1) * AVG
                        ]
        for h in range(2):
            second = lax.dot_general(
                two_ref[...],
                mid[h * 256 : (h + 1) * 256, :],
                (((1,), (1,)), ((), ())),
                preferred_element_type=jnp.float32,
            )
            for c in range(2):
                for b in range(2):
                    for j in range(0, 64, 8):
                        spread[h, c, b, pl.ds(j * PART + i, 8, stride=PART), :] = second[
                            c * 64 + j : c * 64 + j + 8, b * LANES : (b + 1) * LANES
                        ]
        return carry

    lax.fori_loop(0, PART, one_input, 0)
    for h in range(2):
        for c in range(2):
            for b in range(2):
                start = c * 256 + b * LANES
                out_ref[:, h, :, start : start + LANES] = (
                    spread[h, c, b].reshape(64, PART, LANES).astype(jnp.bfloat16)
                )


def spectra(x, taps, consts, tail):
    inputs = x.shape[1]
    one, turn, two = consts
    whole = lambda a: pl.BlockSpec(a.shape, lambda g: (0,) * a.ndim)
    return pl.pallas_call(
        functools.partial(spectra_kernel, tail),
        grid=(inputs // PART,),
        in_specs=[
            pl.BlockSpec((2, PART, F_DEV, ROWS, LANES), lambda g: (0, g, 0, 0, 0)),
            whole(taps),
            whole(one),
            whole(turn),
            whole(two),
        ],
        out_specs=pl.BlockSpec((64, 2, PART, 512), lambda g: (0, 0, g, 0)),
        out_shape=jax.ShapeDtypeStruct((64, 2, inputs, 512), jnp.bfloat16),
        scratch_shapes=[
            pltpu.VMEM((2 * ROWS, F_DEV * LANES), jnp.float32),
            pltpu.VMEM((512, 256), jnp.bfloat16),
            pltpu.VMEM((2, 2, 2, 64 * PART, LANES), jnp.float32),
        ],
        compiler_params=pltpu.CompilerParams(vmem_limit_bytes=48 << 20),
        cost_estimate=pl.CostEstimate(
            flops=4 * 10**9, bytes_accessed=8 << 20, transcendentals=0
        ),
        name="tail" if tail else "head",
    )(x, taps, one, turn, two)


def gram_kernel(info, main_ref, tail_ref, row_ref, col_ref, out_ref, send_ref, left, turned):
    p = pl.program_id(0)

    @pl.when(p == 0)
    def _():
        for t in range(2):
            value = main_ref[:, t]
            if t:
                value = (value.astype(jnp.float32) + tail_ref[:, 0].astype(jnp.float32)).astype(
                    jnp.bfloat16
                )
            value = value.reshape(1024, 512)
            left[:, t * 512 : (t + 1) * 512] = value
            turned[:, t * 512 : t * 512 + 256] = value[:, 256:]
            turned[:, t * 512 + 256 : (t + 1) * 512] = -value[:, :256]

    upper = (p >= 1).astype(jnp.int32) + (p >= 3).astype(jnp.int32) + (p >= 6).astype(jnp.int32)
    lower = p - upper * (upper + 1) // 2
    mine = info[0]
    flag = info[1 + p].astype(jnp.float32) * (1.0 / 512)
    cols = pl.ds(pl.multiple_of(lower * 256, 256), 256)
    right = left[cols, :]
    ids = row_ref[lower]
    for other in range(2):
        half = (1 - mine) if other else mine
        rows = pl.ds(pl.multiple_of(upper * 256 + half * 128, 128), 128)
        weight = jnp.where(col_ref[rows, :] == ids, flag, 0.0)
        for c, source in enumerate((left, turned)):
            product = lax.dot_general(
                source[rows, :],
                right,
                (((1,), (1,)), ((), ())),
                preferred_element_type=jnp.float32,
            )
            if other:
                send_ref[0, c] = (product * weight).astype(jnp.bfloat16)
            else:
                out_ref[0, 0, c] = product * weight


def gram(info, main, tail, row_ids, col_ids):
    stations = main.shape[0]
    return pl.pallas_call(
        gram_kernel,
        grid_spec=pltpu.PrefetchScalarGridSpec(
            num_scalar_prefetch=1,
            grid=(len(PAIRS),),
            in_specs=[
                pl.BlockSpec(main.shape, lambda p, s: (0, 0, 0, 0), pipeline_mode=pl.Buffered(1)),
                pl.BlockSpec(
                    (stations, 1) + tail.shape[2:],
                    lambda p, s: (0, 0, 0, 0),
                    pipeline_mode=pl.Buffered(1),
                ),
                pl.BlockSpec(row_ids.shape, lambda p, s: (0, 0, 0)),
                pl.BlockSpec(col_ids.shape, lambda p, s: (0, 0)),
            ],
            out_specs=[
                pl.BlockSpec((1, 1, 2, 128, 256), lambda p, s: (s[0], p, 0, 0, 0)),
                pl.BlockSpec((1, 2, 128, 256), lambda p, s: (p, 0, 0, 0)),
            ],
            scratch_shapes=[
                pltpu.VMEM((1024, 1024), jnp.bfloat16),
                pltpu.VMEM((1024, 1024), jnp.bfloat16),
            ],
        ),
        out_shape=[
            jax.ShapeDtypeStruct((2, 10, 2, 128, 256), jnp.float32),
            jax.ShapeDtypeStruct((10, 2, 128, 256), jnp.bfloat16),
        ],
        compiler_params=pltpu.CompilerParams(vmem_limit_bytes=48 << 20),
        name="gram",
    )(info, main, tail, row_ids, col_ids)


def fill_kernel(info, whole_ref, got_ref, out_ref):
    out_ref[0] = got_ref[...].astype(jnp.float32)


def fill(info, whole, got):
    return pl.pallas_call(
        fill_kernel,
        grid_spec=pltpu.PrefetchScalarGridSpec(
            num_scalar_prefetch=1,
            grid=(5,),
            in_specs=[
                pl.BlockSpec(memory_space=pl.ANY),
                pl.BlockSpec((2, 2, 128, 256), lambda p, s: (p, 0, 0, 0)),
            ],
            out_specs=pl.BlockSpec((1, 2, 2, 128, 256), lambda p, s: (1 - s[0], p, 0, 0, 0)),
        ),
        out_shape=jax.ShapeDtypeStruct(whole.shape, whole.dtype),
        input_output_aliases={1: 0},
        name="fill",
    )(info, whole, got)


def exchanged(x):
    devices = lax.axis_size("stn") * lax.axis_size("tm")
    flat = x.reshape((devices,) + x.shape[2:])
    return lax.all_to_all(flat, ("stn", "tm"), split_axis=0, concat_axis=0, tiled=True).reshape(
        x.shape
    )


def shards(voltages, filter_taps, membership, block_active):
    inputs = voltages.shape[1]
    mine = lax.axis_index("tm")
    consts = tables()
    x = voltages.reshape(2, inputs, F_DEV, ROWS, LANES)
    taps = filter_taps.reshape(TAPS, ROWS, LANES)
    main = exchanged(spectra(x, taps, consts, False))
    tail = exchanged(spectra(x, taps, consts, True))
    ids = jnp.repeat(lax.dynamic_index_in_dim(membership, mine, 0, keepdims=False), 2)
    flags = lax.dynamic_index_in_dim(block_active, mine, 0, keepdims=False)
    info = jnp.concatenate([mine.astype(jnp.int32)[None], flags])
    whole, send = gram(info, main, tail, ids.reshape(4, 1, 256), ids.reshape(1024, 1))
    got = lax.ppermute(send, "tm", [(0, 1), (1, 0)])
    return fill(info, whole, got)


def solution(mesh):
    placed = (P(None, "stn", "tm"), P(), P("stn", None), P("stn", None))
    return jax.shard_map(
        shards,
        mesh=mesh,
        in_specs=placed,
        out_specs=P("stn", None, None, "tm", None),
        check_vma=False,
    )
```

```python
import jax
import jax.numpy as jnp
import numpy as np
from jax import lax
from jax.experimental import pallas as pl
from jax.experimental.pallas import tpu as pltpu
from jax.sharding import PartitionSpec as P


TAPS = 16
FFT = 4096
LANES = 128
ROWS = FFT // LANES
AVG = 16
F_DEV = 16
PART = 8


def tables():
    q = np.arange(ROWS)
    l = np.arange(LANES)
    angle = 2 * np.pi * np.outer(q, q) / ROWS
    one = np.block([[np.cos(angle), np.sin(angle)], [-np.sin(angle), np.cos(angle)]])
    angle = 2 * np.pi * np.outer(q, l) / FFT
    turn = np.stack([np.cos(angle), -np.sin(angle)])
    angle = 2 * np.pi * np.outer(np.arange(64) - 32, l) / LANES
    two = np.block([[np.cos(angle), np.sin(angle)], [-np.sin(angle), np.cos(angle)]]) / 64
    bf = jnp.bfloat16
    return jnp.asarray(one, bf), jnp.asarray(turn, jnp.float32), jnp.asarray(two, bf)


def head_taps(m):
    return [(t, m - TAPS + 1 + t) for t in range(TAPS) if m - TAPS + 1 + t >= 0]


def tail_taps(m):
    return [(t, m + 1 + t) for t in range(TAPS) if m + 1 + t < F_DEV]


PITCH = 72


def column(m, q):
    return pl.ds(pl.multiple_of(m * FFT + q * LANES, LANES), LANES)


def filtered(choose, x_ref, taps_ref, fir, q, planes):
    w = [jnp.broadcast_to(taps_ref[t : t + 1, column(0, q)], (PART, LANES)) for t in range(TAPS)]
    for n, c in enumerate(planes):
        x = [x_ref[n, :, column(m, q)].astype(jnp.float32) for m in range(F_DEV)]
        for m in range(F_DEV):
            total = jnp.zeros((PART, LANES), jnp.float32)
            for n, (t, frame) in enumerate(choose(m)):
                term = w[t] * x[frame]
                total = total + term if n else term
            fir[m, pl.ds(c * ROWS + q, PART, stride=PITCH), :] = total
        yield


def stage_one(fir, one_ref, turn_ref, mid, i, m):
    rows = pl.ds(pl.multiple_of(i * PITCH, 8), 2 * ROWS)
    frames = jnp.concatenate([fir[m, rows, :], fir[m + 1, rows, :]], axis=1)
    first = jnp.dot(one_ref[...], frames.astype(jnp.bfloat16), preferred_element_type=jnp.float32)
    for k in range(2):
        re = first[:ROWS, k * LANES : (k + 1) * LANES]
        im = first[ROWS:, k * LANES : (k + 1) * LANES]
        parts = (
            re * turn_ref[0] - im * turn_ref[1],
            re * turn_ref[1] + im * turn_ref[0],
        )
        for c in range(2):
            value = parts[c].astype(jnp.bfloat16)
            for h in range(2):
                row = h * 256 + (m + k) * AVG
                mid[row : row + AVG, c * LANES : (c + 1) * LANES] = value[h * AVG : (h + 1) * AVG]


def stage_two(two_ref, mid, spread, i, h):
    second = lax.dot_general(
        two_ref[...],
        mid[h * 256 : (h + 1) * 256, :],
        (((1,), (1,)), ((), ())),
        preferred_element_type=jnp.float32,
    )
    for c in range(2):
        for b in range(2):
            for j in range(0, 64, 8):
                spread[h, c, b, pl.ds(j * PART + i, 8, stride=PART), :] = second[
                    c * 64 + j : c * 64 + j + 8, b * LANES : (b + 1) * LANES
                ]


def put(spread, out_ref):
    for h in range(2):
        for c in range(2):
            for b in range(2):
                start = c * 256 + b * LANES
                out_ref[:, h, :, start : start + LANES] = (
                    spread[h, c, b].reshape(64, PART, LANES).astype(jnp.bfloat16)
                )


def filter_all(choose, x_ref, taps_ref, fir, planes):
    def body(q, carry):
        for _ in filtered(choose, x_ref, taps_ref, fir, q, planes):
            pass
        return carry

    lax.fori_loop(0, ROWS, body, 0)


def transform_all(tables, fir, spread, mids, out_ref, beside=None):
    one_ref, turn_ref, two_ref = tables
    width = 1 if beside else len(mids)

    def body(n, carry):
        other = beside(n) if beside else iter(())
        for m in range(0, F_DEV, 2):
            for k in range(width):
                stage_one(fir, one_ref, turn_ref, mids[k], n * width + k, m)
            next(other, None)
        for h in range(2):
            for k in range(width):
                stage_two(two_ref, mids[k], spread, n * width + k, h)
        for _ in other:
            pass
        return carry

    lax.fori_loop(0, PART // width, body, 0)
    put(spread, out_ref)


def first_kernel(x_ref, taps_ref, *refs):
    tables, (out_ref, fir, spread, *mids) = refs[:3], refs[3:]
    for c in range(2):
        pl.when(pl.program_id(0) == c)(
            lambda: filter_all(head_taps, x_ref, taps_ref, fir, (c,))
        )

    @pl.when(pl.program_id(0) == 1)
    def _():
        transform_all(tables, fir, spread, mids, out_ref)


def rest_kernel(x_ref, taps_ref, *refs):
    tables, (out_ref, fir, spread, *mids) = refs[:3], refs[3:6] + refs[7:]
    pair = (fir, refs[6])
    step = pl.program_id(0)

    @pl.when(step == 0)
    def _():
        filter_all(head_taps, x_ref, taps_ref, pair[0], (0, 1))

    for n in (1, 2):

        @pl.when(step == n)
        def _():
            def beside(i):
                for k in range(4):
                    q = i * 4 + k
                    yield from filtered(tail_taps, x_ref, taps_ref, pair[n % 2], q, (0, 1))

            transform_all(tables, pair[1 - n % 2], spread, mids, out_ref, beside)

    @pl.when(step == 3)
    def _():
        transform_all(tables, pair[0], spread, mids, out_ref)


def spectra(x, taps, consts, first):
    one, turn, two = consts
    steps, outs = (2, 1) if first else (4, 3)
    if first:
        pick = lambda g: (g, 0, 0)
    else:
        pick = lambda g: (0, jnp.where(g == 1, 0, 1), 0)
    whole = lambda a: pl.BlockSpec(a.shape, lambda g: (0,) * a.ndim)
    fir = pltpu.VMEM((F_DEV, PITCH * PART, LANES), jnp.float32)
    return pl.pallas_call(
        first_kernel if first else rest_kernel,
        grid=(steps,),
        in_specs=[
            pl.BlockSpec((1 if first else 2, PART, x.shape[2]), pick),
            whole(taps),
            whole(one),
            whole(turn),
            whole(two),
        ],
        out_specs=pl.BlockSpec((64, 2, PART, 512), lambda g: (0, 0, jnp.maximum(g - 1, 0), 0)),
        out_shape=jax.ShapeDtypeStruct((64, 2, PART * outs, 512), jnp.bfloat16),
        scratch_shapes=[fir, pltpu.VMEM((2, 2, 2, 64 * PART, LANES), jnp.float32)]
        + ([] if first else [fir])
        + [pltpu.VMEM((512, 256), jnp.bfloat16)] * 2,
        compiler_params=pltpu.CompilerParams(vmem_limit_bytes=60 << 20),
        cost_estimate=pl.CostEstimate(
            flops=outs * 2 * 10**9, bytes_accessed=outs * (4 << 20), transcendentals=0
        ),
        name="first" if first else "rest",
    )(x, taps, one, turn, two)


def gram_kernel(first_pair, early_ref, late_ref, late1_ref, row_ref, info, outs, left):
    out_ref, sends = outs[0], outs[1:]
    step = pl.program_id(0)

    @pl.when(step == 0)
    def _():
        for t in range(2):
            for h in range(2):
                rows = slice(h * PART, (h + 1) * PART)
                value = early_ref[:, t] if h == 0 else (late1_ref if t else late_ref)[:, 0, :PART]
                if t:
                    tail = late_ref[:, 0, PART * (1 + h) : PART * (2 + h)]
                    value = value.astype(jnp.float32) + tail.astype(jnp.float32)
                    value = value.astype(jnp.bfloat16)
                for c in range(2):
                    lane = (c * 2 + t) * 256
                    left[:, rows, lane : lane + 256] = value[:, :, c * 256 : (c + 1) * 256]

    pair = step + first_pair
    upper = sum((pair >= edge).astype(jnp.int32) for edge in (1, 3, 6))
    lower = pair - upper * (upper + 1) // 2
    mine = info[0]
    flag = info[1 + pair].astype(jnp.float32) * (1.0 / 512)

    def take(block, lanes):
        return left[block, :, lanes].reshape(-1, 512)

    halves = [pl.ds(upper * 16 + half * 8, 8) for half in (mine, 1 - mine)]
    rows = jnp.concatenate([take(b, lanes) for lanes in PLANES for b in halves], axis=0)
    right = pl.ds(lower * 16, 16)
    by_re, by_im = (
        lax.dot_general(
            rows,
            take(right, lanes),
            (((1,), (1,)), ((), ())),
            preferred_element_type=jnp.float32,
        )
        for lanes in PLANES
    )
    products = (by_re[:256] + by_im[256:], by_re[256:] - by_im[:256])
    ids = row_ref[lower]
    for other in range(2):
        start = pl.multiple_of((1 - mine if other else mine) * 128, 128)
        own = jnp.broadcast_to(row_ref[upper, :, pl.ds(start, 128)], (128, 128)).T
        weight = jnp.where(jnp.concatenate([own, own], axis=1) == ids, flag, 0.0)
        for c in range(2):
            value = products[c][other * 128 : (other + 1) * 128] * weight
            if not other:
                out_ref[0, 0, c] = value
                continue
            value = value.astype(jnp.bfloat16)
            begin = 0
            for send in sends:
                size = send[1]
                if len(sends) == 1:
                    send[0][0, c] = value
                else:

                    @pl.when((step >= begin) & (step < begin + size))
                    def _(ref=send[0]):
                        ref[0, c] = value

                begin += size


PLANES = (slice(0, 512), slice(512, 1024))


def gram(info, early, late, row_ids, first_pair, sizes, blocks, whole=None):
    many = blocks * 16
    aliased = whole is not None

    def kernel(info_ref, *refs):
        refs = refs[aliased:]
        outs = [refs[4]] + list(zip(refs[5 : 5 + len(sizes)], sizes))
        gram_kernel(first_pair, *refs[:4], info_ref, outs, refs[-1])

    def send_spec(begin, size):
        return pl.BlockSpec(
            (1, 2, 128, 256), lambda p, s: (jnp.clip(p - begin, 0, size - 1), 0, 0, 0)
        )

    one = pl.Buffered(1)
    begins = [sum(sizes[:n]) for n in range(len(sizes))]
    count = sum(sizes)
    return pl.pallas_call(
        kernel,
        grid_spec=pltpu.PrefetchScalarGridSpec(
            num_scalar_prefetch=1,
            grid=(count,),
            in_specs=[pl.BlockSpec(memory_space=pl.ANY)] * aliased
            + [
                pl.BlockSpec((many, 2, 8, 512), lambda p, s: (0, 0, 0, 0), pipeline_mode=one),
                pl.BlockSpec((many, 1, 24, 512), lambda p, s: (0, 0, 0, 0), pipeline_mode=one),
                pl.BlockSpec((many, 1, 8, 512), lambda p, s: (0, 1, 0, 0), pipeline_mode=one),
                pl.BlockSpec(row_ids.shape, lambda p, s: (0, 0, 0)),
            ],
            out_specs=[
                pl.BlockSpec(
                    (1, 1, 2, 128, 256), lambda p, s: (s[0], p + first_pair, 0, 0, 0)
                )
            ]
            + [send_spec(b, n) for b, n in zip(begins, sizes)],
            scratch_shapes=[pltpu.VMEM((many, 16, 1024), jnp.bfloat16)],
        ),
        out_shape=[jax.ShapeDtypeStruct((2, 10, 2, 128, 256), jnp.float32)]
        + [jax.ShapeDtypeStruct((n, 2, 128, 256), jnp.bfloat16) for n in sizes],
        input_output_aliases={1: 0} if aliased else {},
        compiler_params=pltpu.CompilerParams(vmem_limit_bytes=24 << 20),
        cost_estimate=pl.CostEstimate(
            flops=count * 27 * 10**7, bytes_accessed=blocks << 20, transcendentals=0
        ),
        name="gram",
    )(info, *([whole] if aliased else []), early, late, late, row_ids)


def fill_kernel(info, whole_ref, got_ref, out_ref):
    out_ref[0] = got_ref[...].astype(jnp.float32)


def fill(info, whole, got, first_pair):
    return pl.pallas_call(
        fill_kernel,
        grid_spec=pltpu.PrefetchScalarGridSpec(
            num_scalar_prefetch=1,
            grid=(got.shape[0],),
            in_specs=[
                pl.BlockSpec(memory_space=pl.ANY),
                pl.BlockSpec((1, 2, 128, 256), lambda p, s: (p, 0, 0, 0)),
            ],
            out_specs=pl.BlockSpec(
                (1, 1, 2, 128, 256), lambda p, s: (1 - s[0], p + first_pair, 0, 0, 0)
            ),
        ),
        out_shape=jax.ShapeDtypeStruct(whole.shape, whole.dtype),
        input_output_aliases={1: 0},
        compiler_params=pltpu.CompilerParams(vmem_limit_bytes=8 << 20),
        cost_estimate=pl.CostEstimate(
            flops=10**5, bytes_accessed=got.shape[0] * 786432, transcendentals=0
        ),
        name="fill",
    )(info, whole, got)


def exchanged(x):
    devices = lax.axis_size("stn") * lax.axis_size("tm")
    flat = x.reshape((devices,) + x.shape[2:])
    return lax.all_to_all(flat, ("stn", "tm"), split_axis=0, concat_axis=0, tiled=True).reshape(
        x.shape
    )


def swapped(x):
    return lax.ppermute(x, "tm", [(0, 1), (1, 0)])


def shards(voltages, filter_taps, membership, block_active):
    mine = lax.axis_index("tm")
    consts = tables()
    early = exchanged(spectra(voltages, filter_taps, consts, True))
    late = exchanged(spectra(voltages, filter_taps, consts, False))
    ids = jnp.repeat(lax.dynamic_index_in_dim(membership, mine, 0, keepdims=False), 2)
    flags = lax.dynamic_index_in_dim(block_active, mine, 0, keepdims=False)
    info = jnp.concatenate([mine.astype(jnp.int32)[None], flags])
    ids = ids.reshape(4, 1, 256)
    whole, send = gram(info, early, late, ids, 0, (3,), 2)
    gots = [swapped(send)]
    whole, *sends = gram(info, early, late, ids, 3, (5, 2), 4, whole)
    gots += [swapped(send) for send in sends]
    for first_pair, got in zip((0, 3, 8), gots):
        whole = fill(info, whole, got, first_pair)
    return whole


def solution(mesh):
    placed = (P(None, "stn", "tm"), P(), P("stn", None), P("stn", None))
    return jax.shard_map(
        shards,
        mesh=mesh,
        in_specs=placed,
        out_specs=P("stn", None, None, "tm", None),
        check_vma=False,
    )
```

```python
import functools
import itertools

import jax
import jax.numpy as jnp
import numpy as np
from jax import lax
from jax.experimental import pallas as pl
from jax.experimental.pallas import tpu as pltpu
from jax.sharding import PartitionSpec as P


TAPS = 16
FFT = 4096
LANES = 128
ROWS = FFT // LANES
AVG = 16
F_DEV = 16
PART = 8


def tables():
    q = np.arange(ROWS)
    l = np.arange(LANES)
    angle = 2 * np.pi * np.outer(q, q) / ROWS
    one = np.block([[np.cos(angle), np.sin(angle)], [-np.sin(angle), np.cos(angle)]])
    angle = 2 * np.pi * np.outer(q, l) / FFT
    turn = np.stack([np.cos(angle), -np.sin(angle)])
    angle = 2 * np.pi * np.outer(np.arange(64) - 32, l) / LANES
    two = np.block([[np.cos(angle), np.sin(angle)], [-np.sin(angle), np.cos(angle)]]) / 64
    bf = jnp.bfloat16
    return jnp.asarray(one, bf), jnp.asarray(turn, jnp.float32), jnp.asarray(two, bf)


HALF = F_DEV // 2


def head_taps(m):
    return [(t, m - TAPS + 1 + t) for t in range(TAPS) if m - TAPS + 1 + t >= 0]


def tail_taps(m):
    return [(t, m + 1 + t) for t in range(TAPS) if m + 1 + t < F_DEV]


LOW_HEAD = (head_taps, 0, range(0, HALF))
HIGH_HEAD = (head_taps, HALF, range(0, F_DEV))
LOW_TAIL = (tail_taps, 0, range(0, F_DEV))
HIGH_TAIL = (tail_taps, HALF, range(HALF, F_DEV))

VMEM_ALL = 67043328
FIRST = ((LOW_HEAD, 0), (LOW_HEAD, 1), (HIGH_TAIL, 0))
REST = ((HIGH_HEAD, 0), (LOW_TAIL, 0), (LOW_TAIL, 1), (HIGH_HEAD, 1), (HIGH_TAIL, 1))


PITCH = 72


def column(m, q):
    return pl.ds(pl.multiple_of(m * FFT + q * LANES, LANES), LANES)


def filtered(kind, origin, x_ref, taps_ref, fir, q):
    choose, start, used = kind
    w = [jnp.broadcast_to(taps_ref[t : t + 1, column(0, q)], (PART, LANES)) for t in range(TAPS)]
    for c in range(2):
        x = {m: x_ref[c, :, column(m - origin, q)].astype(jnp.float32) for m in used}
        for m in range(HALF):
            total = jnp.zeros((PART, LANES), jnp.float32)
            for n, (t, frame) in enumerate(choose(start + m)):
                term = w[t] * x[frame]
                total = total + term if n else term
            fir[m, pl.ds(c * ROWS + q, PART, stride=PITCH), :] = total


def stage_one(fir, one_ref, turn_ref, mid, i, m):
    rows = pl.ds(pl.multiple_of(i * PITCH, 8), 2 * ROWS)
    frames = jnp.concatenate([fir[m, rows, :], fir[m + 1, rows, :]], axis=1)
    first = jnp.dot(one_ref[...], frames.astype(jnp.bfloat16), preferred_element_type=jnp.float32)
    for k in range(2):
        re = first[:ROWS, k * LANES : (k + 1) * LANES]
        im = first[ROWS:, k * LANES : (k + 1) * LANES]
        parts = (
            re * turn_ref[0] - im * turn_ref[1],
            re * turn_ref[1] + im * turn_ref[0],
        )
        for c in range(2):
            value = parts[c].astype(jnp.bfloat16)
            for h in range(2):
                row = h * LANES + (m + k) * AVG
                mid[row : row + AVG, c * LANES : (c + 1) * LANES] = value[h * AVG : (h + 1) * AVG]


def stage_two(two_ref, mid, spread, i):
    second = lax.dot_general(
        two_ref[...],
        mid[...],
        (((1,), (1,)), ((), ())),
        preferred_element_type=jnp.float32,
    )
    for h in range(2):
        for c in range(2):
            for j in range(0, 64, 8):
                spread[h, c, pl.ds(j * PART + i, 8, stride=PART), :] = second[
                    c * 64 + j : c * 64 + j + 8, h * LANES : (h + 1) * LANES
                ]


def filter_all(kind, origin, x_ref, taps_ref, fir):
    together = 4 if len(kind[2]) == HALF else 2

    def body(n, carry):
        for k in range(together):
            filtered(kind, origin, x_ref, taps_ref, fir, n * together + k)
        return carry

    lax.fori_loop(0, ROWS // together, body, 0)


def transform_all(tables, fir, spread, mids, out_ref):
    one_ref, turn_ref, two_ref = tables
    depth = 2
    for i in range(PART + depth):
        if i < PART:
            for m in range(0, HALF, 2):
                stage_one(fir, one_ref, turn_ref, mids[i], i, m)
        if i >= depth:
            stage_two(two_ref, mids[i - depth], spread, i - depth)
    for h in range(2):
        for c in range(2):
            out_ref[:, h, :, c * LANES : (c + 1) * LANES] = (
                spread[h, c].reshape(64, PART, LANES).astype(jnp.bfloat16)
            )


def spectra_kernel(units, width, x_ref, taps_ref, *refs):
    tables, (out_ref, fir, spread, *mids) = refs[:3], refs[3:]
    step = pl.program_id(0)
    for kind in {unit[0]: None for unit in units}:
        here = functools.reduce(
            jnp.logical_or, [step == n for n, unit in enumerate(units) if unit[0] == kind]
        )
        origin = kind[2][0] if width < F_DEV else 0

        @pl.when(here)
        def _():
            filter_all(kind, origin, x_ref, taps_ref, fir)

    transform_all(tables, fir, spread, mids, out_ref)


def listed(values, g):
    return sum(value * (g == n).astype(jnp.int32) for n, value in enumerate(values))


def spectra(x, taps, consts, units):
    one, turn, two = consts
    width = max(len(kind[2]) for kind, _ in units)
    whole = lambda a: pl.BlockSpec(a.shape, lambda g: (0,) * a.ndim)

    def pick(g):
        side = [kind[2][0] // HALF if width < F_DEV else 0 for kind, _ in units]
        return (0, listed([group for _, group in units], g), listed(side, g))

    block = (64, 2, PART, 2 * LANES)
    return pl.pallas_call(
        functools.partial(spectra_kernel, units, width),
        grid=(len(units),),
        in_specs=[
            pl.BlockSpec((2, PART, width * FFT), pick),
            whole(taps),
            whole(one),
            whole(turn),
            whole(two),
        ],
        out_specs=pl.BlockSpec(block, lambda g: (0, 0, 0, g)),
        out_shape=jax.ShapeDtypeStruct(block[:3] + (block[3] * len(units),), jnp.bfloat16),
        scratch_shapes=[
            pltpu.VMEM((HALF, PITCH * PART, LANES), jnp.float32),
            pltpu.VMEM((2, 2, 64 * PART, LANES), jnp.float32),
        ]
        + [pltpu.VMEM((2 * LANES, 2 * LANES), jnp.bfloat16)] * PART,
        compiler_params=pltpu.CompilerParams(vmem_limit_bytes=VMEM_ALL),
        cost_estimate=pl.CostEstimate(
            flops=len(units) * 10**9, bytes_accessed=len(units) << 21, transcendentals=0
        ),
    )(x, taps, one, turn, two)


def gram_kernel(first_pair, early_ref, late_ref, row_ref, info, outs, left):
    out_ref, sends = outs[0], outs[1:]
    step = pl.program_id(0)

    def arrived(kind, group, t, c):
        ref, units = (early_ref, FIRST) if (kind, group) in FIRST else (late_ref, REST)
        lane = (units.index((kind, group)) * 2 + c) * LANES
        return ref[:, t, :, lane : lane + LANES]

    @pl.when(step == 0)
    def _():
        kinds = ((LOW_HEAD, LOW_TAIL), (HIGH_HEAD, HIGH_TAIL))
        for c, t, h, group in itertools.product(range(2), repeat=4):
            head, tail = kinds[h]
            value = arrived(head, group, t, c)
            if t:
                more = arrived(tail, group, 0, c).astype(jnp.float32)
                value = (value.astype(jnp.float32) + more).astype(jnp.bfloat16)
            lane = (c * 4 + t * 2 + h) * LANES
            left[:, group * PART : (group + 1) * PART, lane : lane + LANES] = value

    pair = step + first_pair
    upper = sum((pair >= edge).astype(jnp.int32) for edge in (1, 3, 6))
    lower = pair - upper * (upper + 1) // 2
    mine = info[0]
    flag = info[1 + pair].astype(jnp.float32) * (1.0 / 512)

    def take(block, lanes):
        return left[block, :, lanes].reshape(-1, 512)

    halves = [pl.ds(upper * 16 + half * 8, 8) for half in (mine, 1 - mine)]
    rows = jnp.concatenate([take(b, lanes) for lanes in PLANES for b in halves], axis=0)
    right = pl.ds(lower * 16, 16)
    by_re, by_im = (
        lax.dot_general(
            rows,
            take(right, lanes),
            (((1,), (1,)), ((), ())),
            preferred_element_type=jnp.float32,
        )
        for lanes in PLANES
    )
    products = (by_re[:256] + by_im[256:], by_re[256:] - by_im[:256])
    ids = row_ref[lower]
    for other in range(2):
        start = pl.multiple_of((1 - mine if other else mine) * 128, 128)
        own = jnp.broadcast_to(row_ref[upper, :, pl.ds(start, 128)], (128, 128)).T
        weight = jnp.where(jnp.concatenate([own, own], axis=1) == ids, flag, 0.0)
        for c in range(2):
            value = products[c][other * 128 : (other + 1) * 128] * weight
            if not other:
                out_ref[0, 0, c] = value
                continue
            value = value.astype(jnp.bfloat16)
            begin = 0
            for send in sends:
                size = send[1]
                if len(sends) == 1:
                    send[0][0, c] = value
                else:

                    @pl.when((step >= begin) & (step < begin + size))
                    def _(ref=send[0]):
                        ref[0, c] = value

                begin += size


PLANES = (slice(0, 512), slice(512, 1024))


def gram(info, early, late, row_ids, first_pair, sizes, blocks, whole=None):
    many = blocks * 16
    aliased = whole is not None

    def kernel(info_ref, *refs):
        refs = refs[aliased:]
        outs = [refs[3]] + list(zip(refs[4 : 4 + len(sizes)], sizes))
        gram_kernel(first_pair, *refs[:3], info_ref, outs, refs[-1])

    def send_spec(begin, size):
        return pl.BlockSpec(
            (1, 2, 128, 256), lambda p, s: (jnp.clip(p - begin, 0, size - 1), 0, 0, 0)
        )

    one = pl.Buffered(1)
    begins = [sum(sizes[:n]) for n in range(len(sizes))]
    count = sum(sizes)
    return pl.pallas_call(
        kernel,
        grid_spec=pltpu.PrefetchScalarGridSpec(
            num_scalar_prefetch=1,
            grid=(count,),
            in_specs=[pl.BlockSpec(memory_space=pl.ANY)] * aliased
            + [
                pl.BlockSpec(
                    (many,) + x.shape[1:], lambda p, s: (0, 0, 0, 0), pipeline_mode=one
                )
                for x in (early, late)
            ]
            + [
                pl.BlockSpec(row_ids.shape, lambda p, s: (0, 0, 0)),
            ],
            out_specs=[
                pl.BlockSpec(
                    (1, 1, 2, 128, 256), lambda p, s: (s[0], p + first_pair, 0, 0, 0)
                )
            ]
            + [send_spec(b, n) for b, n in zip(begins, sizes)],
            scratch_shapes=[pltpu.VMEM((many, 16, 1024), jnp.bfloat16)],
        ),
        out_shape=[jax.ShapeDtypeStruct((2, 10, 2, 128, 256), jnp.float32)]
        + [jax.ShapeDtypeStruct((n, 2, 128, 256), jnp.bfloat16) for n in sizes],
        input_output_aliases={1: 0} if aliased else {},
        compiler_params=pltpu.CompilerParams(vmem_limit_bytes=24 << 20),
        cost_estimate=pl.CostEstimate(
            flops=count * 27 * 10**7, bytes_accessed=blocks << 20, transcendentals=0
        ),
        name="gram",
    )(info, *([whole] if aliased else []), early, late, row_ids)


def fill_kernel(info, whole_ref, got_ref, out_ref):
    out_ref[0] = got_ref[...].astype(jnp.float32)


def fill(info, whole, got, first_pair):
    return pl.pallas_call(
        fill_kernel,
        grid_spec=pltpu.PrefetchScalarGridSpec(
            num_scalar_prefetch=1,
            grid=(got.shape[0],),
            in_specs=[
                pl.BlockSpec(memory_space=pl.ANY),
                pl.BlockSpec((1, 2, 128, 256), lambda p, s: (p, 0, 0, 0)),
            ],
            out_specs=pl.BlockSpec(
                (1, 1, 2, 128, 256), lambda p, s: (1 - s[0], p + first_pair, 0, 0, 0)
            ),
        ),
        out_shape=jax.ShapeDtypeStruct(whole.shape, whole.dtype),
        input_output_aliases={1: 0},
        compiler_params=pltpu.CompilerParams(vmem_limit_bytes=8 << 20),
        cost_estimate=pl.CostEstimate(
            flops=10**5, bytes_accessed=got.shape[0] * 786432, transcendentals=0
        ),
        name="fill",
    )(info, whole, got)


def exchanged(x):
    devices = lax.axis_size("stn") * lax.axis_size("tm")
    flat = x.reshape((devices,) + x.shape[2:])
    flat = lax.all_to_all(flat, ("stn", "tm"), split_axis=0, concat_axis=0, tiled=True)
    return flat.reshape(x.shape)


def swapped(x):
    return lax.ppermute(x, "tm", [(0, 1), (1, 0)])


def shards(voltages, filter_taps, membership, block_active):
    mine = lax.axis_index("tm")
    consts = tables()
    ids = jnp.repeat(lax.dynamic_index_in_dim(membership, mine, 0, keepdims=False), 2)
    flags = lax.dynamic_index_in_dim(block_active, mine, 0, keepdims=False)
    info = jnp.concatenate([mine.astype(jnp.int32)[None], flags])
    ids = ids.reshape(4, 1, 256)
    early = exchanged(spectra(voltages, filter_taps, consts, FIRST))
    late = spectra(voltages, filter_taps, consts, REST)
    late = exchanged(late)
    whole, send = gram(info, early, late, ids, 0, (3,), 2)
    gots = [swapped(send)]
    whole, *sends = gram(info, early, late, ids, 3, (5, 2), 4, whole)
    gots += [swapped(send) for send in sends]
    for first_pair, got in zip((0, 3, 8), gots):
        whole = fill(info, whole, got, first_pair)
    return whole


def solution(mesh):
    placed = (P(None, "stn", "tm"), P(), P("stn", None), P("stn", None))
    return jax.shard_map(
        shards,
        mesh=mesh,
        in_specs=placed,
        out_specs=P("stn", None, None, "tm", None),
        check_vma=False,
    )
```

```python
import functools
import itertools

import jax
import jax.numpy as jnp
import numpy as np
from jax import lax
from jax.experimental import pallas as pl
from jax.experimental.pallas import tpu as pltpu
from jax.sharding import PartitionSpec as P


TAPS = 16
FFT = 4096
LANES = 128
ROWS = FFT // LANES
AVG = 16
F_DEV = 16
PART = 8


def tables():
    q = np.arange(ROWS)
    l = np.arange(LANES)
    angle = 2 * np.pi * np.outer(q, q) / ROWS
    one = np.block([[np.cos(angle), np.sin(angle)], [-np.sin(angle), np.cos(angle)]])
    angle = 2 * np.pi * np.outer(q, l) / FFT
    turn = np.stack([np.cos(angle), -np.sin(angle)])
    angle = 2 * np.pi * np.outer(np.arange(64) - 32, l) / LANES
    two = np.block([[np.cos(angle), np.sin(angle)], [-np.sin(angle), np.cos(angle)]]) / 64
    bf = jnp.bfloat16
    return jnp.asarray(one, bf), jnp.asarray(turn, jnp.float32), jnp.asarray(two, bf)


HALF = F_DEV // 2


def head_taps(m):
    return [(t, m - TAPS + 1 + t) for t in range(TAPS) if m - TAPS + 1 + t >= 0]


def tail_taps(m):
    return [(t, m + 1 + t) for t in range(TAPS) if m + 1 + t < F_DEV]


LOW_HEAD = (head_taps, 0, range(0, HALF))
HIGH_HEAD = (head_taps, HALF, range(0, F_DEV))
LOW_TAIL = (tail_taps, 0, range(0, F_DEV))
HIGH_TAIL = (tail_taps, HALF, range(HALF, F_DEV))

VMEM_ALL = 67043328
FIRST = ((LOW_HEAD, 0), (LOW_HEAD, 1), (HIGH_TAIL, 0))
REST = ((HIGH_HEAD, 0), (LOW_TAIL, 0), (LOW_TAIL, 1), (HIGH_HEAD, 1), (HIGH_TAIL, 1))


PITCH = 72


def column(m, q):
    return pl.ds(pl.multiple_of(m * FFT + q * LANES, LANES), LANES)


def filtered(kind, origin, x_ref, taps_ref, fir, q):
    choose, start, used = kind
    w = [jnp.broadcast_to(taps_ref[t : t + 1, column(0, q)], (PART, LANES)) for t in range(TAPS)]
    for c in range(2):
        x = {m: x_ref[c, :, column(m - origin, q)].astype(jnp.float32) for m in used}
        for m in range(HALF):
            total = jnp.zeros((PART, LANES), jnp.float32)
            for n, (t, frame) in enumerate(choose(start + m)):
                term = w[t] * x[frame]
                total = total + term if n else term
            fir[m, pl.ds(c * ROWS + q, PART, stride=PITCH), :] = total


def stage_one(fir, one_ref, turn_ref, mid, i, m):
    rows = pl.ds(pl.multiple_of(i * PITCH, 8), 2 * ROWS)
    frames = jnp.concatenate([fir[m, rows, :], fir[m + 1, rows, :]], axis=1)
    first = jnp.dot(one_ref[...], frames.astype(jnp.bfloat16), preferred_element_type=jnp.float32)
    for k in range(2):
        re = first[:ROWS, k * LANES : (k + 1) * LANES]
        im = first[ROWS:, k * LANES : (k + 1) * LANES]
        parts = (
            re * turn_ref[0] - im * turn_ref[1],
            re * turn_ref[1] + im * turn_ref[0],
        )
        for c in range(2):
            value = parts[c].astype(jnp.bfloat16)
            for h in range(2):
                row = h * LANES + (m + k) * AVG
                mid[row : row + AVG, c * LANES : (c + 1) * LANES] = value[h * AVG : (h + 1) * AVG]


def stage_two(two_ref, mid, spread, i):
    second = lax.dot_general(
        two_ref[...],
        mid[...],
        (((1,), (1,)), ((), ())),
        preferred_element_type=jnp.float32,
    )
    for h in range(2):
        for c in range(2):
            for j in range(0, 64, 8):
                spread[h, c, pl.ds(j * PART + i, 8, stride=PART), :] = second[
                    c * 64 + j : c * 64 + j + 8, h * LANES : (h + 1) * LANES
                ]


def filter_all(kind, origin, x_ref, taps_ref, fir):
    together = 4 if len(kind[2]) == HALF else 2

    def body(n, carry):
        for k in range(together):
            filtered(kind, origin, x_ref, taps_ref, fir, n * together + k)
        return carry

    lax.fori_loop(0, ROWS // together, body, 0)


def transform_all(tables, fir, spread, mids, out_ref):
    one_ref, turn_ref, two_ref = tables
    depth = 5
    for i in range(PART + depth):
        if i < PART:
            for m in range(0, HALF, 2):
                stage_one(fir, one_ref, turn_ref, mids[i], i, m)
        if i >= depth:
            stage_two(two_ref, mids[i - depth], spread, i - depth)
    for h in range(2):
        for c in range(2):
            out_ref[:, h, :, c * LANES : (c + 1) * LANES] = (
                spread[h, c].reshape(64, PART, LANES).astype(jnp.bfloat16)
            )


def spectra_kernel(units, width, x_ref, taps_ref, *refs):
    tables, (out_ref, fir, spread, *mids) = refs[:3], refs[3:]
    step = pl.program_id(0)
    for kind in {unit[0]: None for unit in units}:
        here = functools.reduce(
            jnp.logical_or, [step == n for n, unit in enumerate(units) if unit[0] == kind]
        )
        origin = kind[2][0] if width < F_DEV else 0

        @pl.when(here)
        def _():
            filter_all(kind, origin, x_ref, taps_ref, fir)

    transform_all(tables, fir, spread, mids, out_ref)


def listed(values, g):
    return sum(value * (g == n).astype(jnp.int32) for n, value in enumerate(values))


def spectra(x, taps, consts, units):
    one, turn, two = consts
    width = max(len(kind[2]) for kind, _ in units)
    whole = lambda a: pl.BlockSpec(a.shape, lambda g: (0,) * a.ndim)

    def pick(g):
        side = [kind[2][0] // HALF if width < F_DEV else 0 for kind, _ in units]
        return (0, listed([group for _, group in units], g), listed(side, g))

    block = (64, 2, PART, 2 * LANES)
    return pl.pallas_call(
        functools.partial(spectra_kernel, units, width),
        grid=(len(units),),
        in_specs=[
            pl.BlockSpec((2, PART, width * FFT), pick),
            whole(taps),
            whole(one),
            whole(turn),
            whole(two),
        ],
        out_specs=pl.BlockSpec(block, lambda g: (0, 0, 0, g)),
        out_shape=jax.ShapeDtypeStruct(block[:3] + (block[3] * len(units),), jnp.bfloat16),
        scratch_shapes=[
            pltpu.VMEM((HALF, PITCH * PART, LANES), jnp.float32),
            pltpu.VMEM((2, 2, 64 * PART, LANES), jnp.float32),
        ]
        + [pltpu.VMEM((2 * LANES, 2 * LANES), jnp.bfloat16)] * PART,
        compiler_params=pltpu.CompilerParams(vmem_limit_bytes=VMEM_ALL),
        cost_estimate=pl.CostEstimate(
            flops=len(units) * 10**9, bytes_accessed=len(units) << 21, transcendentals=0
        ),
    )(x, taps, one, turn, two)


def blocks_of(pair):
    upper = sum((pair >= edge).astype(jnp.int32) for edge in (1, 3, 6))
    return upper, pair - upper * (upper + 1) // 2


def plane_of(pair):
    if isinstance(pair, int):
        return 4 * pair - sum(pair > edge for edge in (0, 2, 5, 9))
    return 4 * pair - sum((pair > edge).astype(jnp.int32) for edge in (0, 2, 5, 9))


def triangle():
    rows = lax.broadcasted_iota(jnp.int32, (LANES, LANES), 0)
    return rows - lax.broadcasted_iota(jnp.int32, (LANES, LANES), 1)


def pack(send_ref, at, values, mine, diagonal):
    @pl.when(diagonal)
    def _():
        sides = [(v[:, :LANES], v[:, LANES:]) for v in values]
        own = [jnp.where(mine == 0, x, y) for x, y in sides]
        square = [jnp.where(mine == 0, y, x) for x, y in sides]
        send_ref[at] = own[0].astype(jnp.bfloat16)
        send_ref[at + 1] = own[1].astype(jnp.bfloat16)
        send_ref[at + 2] = jnp.where(triangle() >= 0, *square).astype(jnp.bfloat16)

    @pl.when(jnp.logical_not(diagonal))
    def _():
        for c in range(2):
            for k in range(2):
                side = values[c][:, k * LANES : (k + 1) * LANES]
                send_ref[at + 2 * c + k] = side.astype(jnp.bfloat16)


def gram_kernel(
    first_pair, sizes, begin_s, early_ref, late_ref, row_ref, info, out_ref, sends, left, done_ref
):
    step = pl.program_id(0)

    def arrived(kind, group, t, c):
        sent = (kind, group) in FIRST
        lane = ((FIRST if sent else REST).index((kind, group)) * 2 + c) * LANES
        lanes = slice(lane, lane + LANES)
        return early_ref[:, t, :, lanes] if sent else late_ref[begin_s : left.shape[0], t, :, lanes]

    @pl.when(step == 0)
    def _():
        kinds = ((LOW_HEAD, LOW_TAIL), (HIGH_HEAD, HIGH_TAIL))
        for c, t, h, group in itertools.product(range(2), repeat=4):
            head, tail = kinds[h]
            value = arrived(head, group, t, c)
            if t:
                more = arrived(tail, group, 0, c).astype(jnp.float32)
                value = (value.astype(jnp.float32) + more).astype(jnp.bfloat16)
            lane = (c * 4 + t * 2 + h) * LANES
            left[begin_s:, group * PART : (group + 1) * PART, lane : lane + LANES] = value
        if begin_s:
            left[:begin_s] = done_ref[...]

    pair = step + first_pair
    upper, lower = blocks_of(pair)
    mine = info[0]
    flag = info[1 + pair].astype(jnp.float32) * (1.0 / 512)

    def take(block, lanes):
        return left[block, :, lanes].reshape(-1, 512)

    halves = [pl.ds(upper * 16 + half * 8, 8) for half in (mine, 1 - mine)]
    rows = jnp.concatenate([take(b, lanes) for lanes in PLANES for b in halves], axis=0)
    right = pl.ds(lower * 16, 16)
    by_re, by_im = (
        lax.dot_general(
            rows,
            take(right, lanes),
            (((1,), (1,)), ((), ())),
            preferred_element_type=jnp.float32,
        )
        for lanes in PLANES
    )
    products = (by_re[:256] + by_im[256:], by_re[256:] - by_im[:256])
    ids = row_ref[lower]
    values = []
    for other in range(2):
        start = pl.multiple_of((1 - mine if other else mine) * 128, 128)
        own = jnp.broadcast_to(row_ref[upper, :, pl.ds(start, 128)], (128, 128)).T
        weight = jnp.where(jnp.concatenate([own, own], axis=1) == ids, flag, 0.0)
        values.append([x[other * 128 : (other + 1) * 128] * weight for x in products])
    for c in range(2):
        out_ref[0, 0, c] = values[0][c]
    begin = first_pair
    for send_ref, size in zip(sends, sizes):
        inside = (pair >= begin) & (pair < begin + size)
        at = plane_of(pair) - plane_of(begin)
        pl.when(inside)(
            functools.partial(pack, send_ref, at, values[1], mine, upper == lower)
        )
        begin += size


PLANES = (slice(0, 512), slice(512, 1024))
SIZES = (3, 5, 2)


IN_VMEM = pl.BlockSpec(memory_space=pltpu.VMEM)


def gram(info, early, late, row_ids, first_pair, sizes, blocks, whole=None, done=None):
    many = blocks * 16
    more = whole is not None
    begin_s = done.shape[0] if more else 0
    fresh = many - begin_s
    begins = [first_pair + sum(sizes[:n]) for n in range(len(sizes))]
    planes = [plane_of(b + n) - plane_of(b) for b, n in zip(begins, sizes)]
    count = sum(sizes)
    rows = (many, 16, 1024)

    def kernel(info_ref, *refs):
        done_ref = refs[1] if more else None
        refs = refs[2 * more :]
        gram_kernel(
            first_pair, sizes, begin_s, *refs[:3], info_ref, refs[3], refs[4:-1], refs[-1], done_ref
        )

    outs = [jax.ShapeDtypeStruct((2, 10, 2, 128, 256), jnp.float32)] + [
        jax.ShapeDtypeStruct((n, LANES, LANES), jnp.bfloat16) for n in planes
    ]
    return pl.pallas_call(
        kernel,
        grid_spec=pltpu.PrefetchScalarGridSpec(
            num_scalar_prefetch=1,
            grid=(count,),
            in_specs=[pl.BlockSpec(memory_space=pl.ANY), IN_VMEM][: 2 * more]
            + [
                pl.BlockSpec(
                    (fresh,) + early.shape[1:],
                    lambda p, s: (begin_s // fresh, 0, 0, 0),
                    pipeline_mode=pl.Buffered(1),
                ),
                IN_VMEM,
                pl.BlockSpec(row_ids.shape, lambda p, s: (0, 0, 0)),
            ],
            out_specs=[
                pl.BlockSpec(
                    (1, 1, 2, 128, 256), lambda p, s: (s[0], p + first_pair, 0, 0, 0)
                )
            ]
            + [IN_VMEM] * (len(sizes) + (not more)),
            scratch_shapes=[pltpu.VMEM(rows, jnp.bfloat16)] if more else [],
        ),
        out_shape=outs + ([] if more else [jax.ShapeDtypeStruct(rows, jnp.bfloat16)]),
        input_output_aliases={1: 0} if more else {},
        compiler_params=pltpu.CompilerParams(vmem_limit_bytes=24 << 20),
        cost_estimate=pl.CostEstimate(
            flops=count * 27 * 10**7, bytes_accessed=blocks << 20, transcendentals=0
        ),
        name="gram",
    )(info, *([whole, done] if more else []), early, late, row_ids)


def fill_kernel(first_pair, info, whole_ref, got_ref, out_ref):
    pair = pl.program_id(0) + first_pair
    upper, lower = blocks_of(pair)
    mine = info[0]
    at = plane_of(pair) - plane_of(first_pair)

    @pl.when(upper == lower)
    def _():
        own = pl.ds(pl.multiple_of(mine * LANES, LANES), LANES)
        far = pl.ds(pl.multiple_of((1 - mine) * LANES, LANES), LANES)
        packed = got_ref[at + 2].astype(jnp.float32)
        turned = packed.T
        below = triangle()
        out_ref[0, 0, 0, :, own] = jnp.where(below >= 0, packed, turned)
        out_ref[0, 0, 1, :, own] = jnp.where(
            below < 0, packed, jnp.where(below > 0, -turned, 0.0)
        )
        for c in range(2):
            out_ref[0, 0, c, :, far] = got_ref[at + c].astype(jnp.float32)

    @pl.when(upper != lower)
    def _():
        for c in range(2):
            for k in range(2):
                out_ref[0, 0, c, :, k * LANES : (k + 1) * LANES] = got_ref[
                    at + 2 * c + k
                ].astype(jnp.float32)


def fill(info, whole, got, first_pair, count):
    return pl.pallas_call(
        functools.partial(fill_kernel, first_pair),
        grid_spec=pltpu.PrefetchScalarGridSpec(
            num_scalar_prefetch=1,
            grid=(count,),
            in_specs=[
                pl.BlockSpec(memory_space=pl.ANY),
                pl.BlockSpec(memory_space=pltpu.VMEM),
            ],
            out_specs=pl.BlockSpec(
                (1, 1, 2, 128, 256), lambda p, s: (1 - s[0], p + first_pair, 0, 0, 0)
            ),
        ),
        out_shape=jax.ShapeDtypeStruct(whole.shape, whole.dtype),
        input_output_aliases={1: 0},
        compiler_params=pltpu.CompilerParams(vmem_limit_bytes=8 << 20),
        cost_estimate=pl.CostEstimate(
            flops=10**5, bytes_accessed=count * 786432, transcendentals=0
        ),
        name="fill",
    )(info, whole, got)


def exchanged(x):
    devices = lax.axis_size("stn") * lax.axis_size("tm")
    flat = x.reshape((devices,) + x.shape[2:])
    flat = lax.all_to_all(flat, ("stn", "tm"), split_axis=0, concat_axis=0, tiled=True)
    return flat.reshape(x.shape)


def swapped(x):
    return lax.ppermute(x, "tm", [(0, 1), (1, 0)])


def shards(voltages, filter_taps, membership, block_active):
    mine = lax.axis_index("tm")
    consts = tables()
    ids = jnp.repeat(lax.dynamic_index_in_dim(membership, mine, 0, keepdims=False), 2)
    flags = lax.dynamic_index_in_dim(block_active, mine, 0, keepdims=False)
    info = jnp.concatenate([mine.astype(jnp.int32)[None], flags])
    ids = ids.reshape(4, 1, 256)
    early = exchanged(spectra(voltages, filter_taps, consts, FIRST))
    late = spectra(voltages, filter_taps, consts, REST)
    late = exchanged(late)
    whole, send, done = gram(info, early, late, ids, 0, SIZES[:1], 2)
    gots = [swapped(send)]
    whole, *sends = gram(
        info, early, late, ids, SIZES[0], SIZES[1:], 4, whole, done
    )
    gots += [swapped(send) for send in sends]
    for n, got in enumerate(gots):
        whole = fill(info, whole, got, sum(SIZES[:n]), SIZES[n])
    return whole


def solution(mesh):
    placed = (P(None, "stn", "tm"), P(), P("stn", None), P("stn", None))
    return jax.shard_map(
        shards,
        mesh=mesh,
        in_specs=placed,
        out_specs=P("stn", None, None, "tm", None),
        check_vma=False,
    )
```
